128 devices in a mesh: slab: 32 (over z, y, x_hi), chan: 4 (over x_lo, core).
Axes of the slice: x: 4 (x_hi: 2, x_lo: 2; x = x_hi * 2 + x_lo), y: 4, z: 4, core: 2. Of those that a mesh axis runs over, the one named last changes fastest.
Arguments:
- volume: bfloat16 [2, 128, 128, 32, 128], P(None, 'slab', 'chan'), may hold values from -6 to 6
- first_kernel: bfloat16 [3, 3, 3, 128, 128], P(None, None, None, None, 'chan'), may hold values from -0.109375 to 0.109375
- first_bias: float32 [128], P('chan'), may hold values from -3 to 3
- second_kernel: bfloat16 [3, 3, 3, 128, 128], P(None, None, None, 'chan'), may hold values from -0.109375 to 0.109375
- second_bias: float32 [128], P('chan'), may hold values from -3 to 3
Outputs:
- features_out: bfloat16 [2, 128, 128, 32, 128], P(None, 'slab', 'chan')
The draws below stay inside these ranges and needn't reach their ends.
All inputs are finite; a program needn't handle non-finite values.
Results may differ from the reference program's by a relative error of at most 0.0046.
Values may be sent and summed in bfloat16 or wider, within the bound.
A program may use at most 128 MiB of HBM per device.

```python
import jax
import jax.numpy as jnp
from jax import lax

C = 128
BATCH = 2
THICK = 32
NY = 128
DEPTH = 128


def levels(own_key, dims, pieces, smallest, high):
    gain = 1.0
    for axis_at, shards_of in pieces:
        draws = jax.random.uniform(jax.random.fold_in(jax.random.fold_in(own_key, 6), axis_at), (shards_of,), jnp.float32, smallest / len(pieces), high / len(pieces))
        gain = gain * jnp.repeat(jnp.exp(draws), dims[axis_at] // shards_of).reshape((-1,) + (1,) * (len(dims) - 1 - axis_at))
    return gain


def scatter_about(stream_key, extent, spread, reach, shards=(), held_as=jnp.bfloat16):
    values = spread * jax.random.normal(stream_key, extent, jnp.float32)
    if shards:
        values = values * levels(stream_key, extent, shards, -0.22, 0.18)
    return jnp.clip(values, -reach, reach).astype(held_as)


def setup_inputs(seed: int = 0) -> dict:
    streams_of = jax.random.split(jax.random.key(seed), 6)
    return {
        "volume": scatter_about(streams_of[0], (BATCH, DEPTH, C, THICK, NY), 1.0, 6.0, ((1, 32), (2, 4))),
        "first_kernel": scatter_about(streams_of[1], (3, 3, 3, C, C), (27 * C) ** -0.5, 0.109375, ((4, 4),)),
        "first_bias": scatter_about(streams_of[2], (C,), 0.5, 3.0, ((0, 4),), jnp.float32),
        "second_kernel": scatter_about(streams_of[3], (3, 3, 3, C, C), (27 * C) ** -0.5, 0.109375, ((3, 4),)),
        "second_bias": scatter_about(streams_of[4], (C,), 0.5, 3.0, ((0, 4),), jnp.float32),
    }


layout_spec = ("NDCHW", "DHWIO", "NDCHW")


def conv_layer(values_in, kernel, bias_row):
    summed = lax.conv_general_dilated(values_in.astype(jnp.float32), kernel.astype(jnp.float32), (1, 1, 1), ((1, 1), (1, 1), (1, 1)), dimension_numbers=layout_spec, precision=lax.Precision.HIGHEST)
    return jax.nn.relu(summed + bias_row.astype(jnp.float32)[None, None, :, None, None]).astype(jnp.bfloat16)


def reference(volume, first_kernel, first_bias, second_kernel, second_bias):
    hidden = conv_layer(volume, first_kernel, first_bias)
    return conv_layer(hidden, second_kernel, second_bias)
```

```python
import jax
import jax.numpy as jnp
from jax import lax
from jax.experimental import pallas as pl
from jax.experimental.pallas import tpu as pltpu
from jax.sharding import PartitionSpec as P

MESH = pl.DeviceIdType.MESH
SLABS = 32
BF16 = jnp.bfloat16
F32 = jnp.float32
LAYERS = (0, 1, 2, 3)


def conv_rows(source, layer, row, weights, bias):
    taps = [
        jnp.concatenate([source[layer + a, row + c], source[layer + a, row + c + 1]], axis=1)
        for a in range(3)
        for c in range(3)
    ]
    sums = jnp.dot(weights, jnp.concatenate(taps, axis=0), preferred_element_type=F32)
    lane = lax.broadcasted_iota(jnp.int32, (128, 128), 1)
    outs = []
    for r in range(2):
        cols = slice(128 * r, 128 * r + 128)
        left = jnp.where(lane == 0, 0.0, pltpu.roll(sums[0:128, cols], 1, 1))
        right = jnp.where(lane == 127, 0.0, pltpu.roll(sums[256:384, cols], 127, 1))
        outs.append(jnp.maximum(sums[128:256, cols] + left + right + bias, 0.0).astype(BF16))
    return outs


def stacked(taps):
    return jnp.concatenate([taps[3 * j : 3 * j + 3].reshape(384, 128) for j in range(9)], axis=1)


def kernel(
    vol, w1_in, w2_in, bias_in, out,
    landed, given, shared, x, hid, res, back, final, w1, w2, w2t, bias,
    sem_vol, sem_w, w_send, w_recv, x_send, x_recv, t_send, t_recv, z_send, z_recv, o_send, o_recv, o_self, sem_out,
):
    s = lax.axis_index("slab")
    k = lax.axis_index("chan")
    core = lax.rem(k, 2)
    chip = k // 2
    other = 1 - core
    sib = 2 * chip + other
    across = 2 * (1 - chip) + core
    diag = 2 * (1 - chip) + other
    mine = lax.rem(chip + s, 2)
    theirs = 1 - mine
    up, down = lax.rem(s + 1, SLABS), lax.rem(s + SLABS - 1, SLABS)
    pair = s + 1 - 2 * lax.rem(s, 2)
    has_down, has_up = s > 0, s < SLABS - 1
    ch = pl.ds(pl.multiple_of(k * 32, 32), 32)
    near_ch = pl.ds(pl.multiple_of(chip * 64, 64), 64)
    far_ch = pl.ds(pl.multiple_of((1 - chip) * 64, 64), 64)

    def remote(src, dst, send, recv, slab, chan):
        return pltpu.make_async_remote_copy(
            src_ref=src, dst_ref=dst, send_sem=send, recv_sem=recv, device_id=(slab, chan), device_id_type=MESH
        )

    barrier = pltpu.get_barrier_semaphore()
    for slab, chan in ((s, sib), (s, across), (s, diag), (up, across), (down, across)):
        pl.semaphore_signal(barrier, inc=1, device_id=(slab, chan), device_id_type=MESH)

    vol_copy = {}
    for z in LAYERS:
        for which, b in ((1, theirs), (0, mine)):
            vol_copy[which, z] = pltpu.make_async_copy(vol.at[b, z], landed.at[which, z], sem_vol.at[which, z])
            vol_copy[which, z].start()
    gathers = ((bias_in, bias), (w1_in, w1), (w2_in, w2))
    own_w = []
    for n, (src, dst) in enumerate(gathers):
        own_w.append(pltpu.make_async_copy(src, dst.at[:, ch, :], sem_w.at[n]))
        own_w[n].start()

    edge = 18 * core
    blank = jnp.zeros((2, 128, 128), BF16)

    def blank_rows(i, carry):
        x[i, pl.ds(edge, 2)] = blank
        return carry

    lax.fori_loop(0, 8, blank_rows, 0)

    def blank_layer(ref, layer, rows):
        def row(i, carry):
            ref[layer, i] = jnp.zeros((128, 128), BF16)
            return carry

        lax.fori_loop(0, rows, row, 0)

    @pl.when(jnp.logical_not(has_down))
    def _():
        blank_layer(x, 1, 20)
        blank_layer(hid, 0, 18)

    @pl.when(jnp.logical_not(has_up))
    def _():
        blank_layer(x, 6, 20)
        blank_layer(hid, 5, 18)

    pl.semaphore_wait(barrier, 5)

    def w_copy(n, i, chan_from, slab, chan):
        ref = gathers[n][1]
        part = ref.at[:, pl.ds(pl.multiple_of(chan_from * 32, 32), 32), :]
        return remote(part, part, w_send.at[n, i], w_recv.at[n, i], slab, chan)

    def start_w(n):
        own_w[n].wait()
        w_copy(n, 0, k, s, sib).start()
        w_copy(n, 1, k, pair, across).start()

    def pass_w(n):
        w_copy(n, 1, across, pair, across).wait_recv()
        w_copy(n, 2, across, s, sib).start()

    def end_w(n):
        w_copy(n, 0, sib, s, sib).wait_recv()
        w_copy(n, 2, diag, s, sib).wait_recv()

    def x_copy(z, i):
        rows = pl.ds(2, 16)
        if i == 0:
            return remote(shared.at[z], x.at[z + 2, rows, ch, :], x_send.at[z, 0], x_recv.at[z, 0], s, sib)
        half, chan = ((core, across), (other, diag))[i - 1]
        return remote(
            given.at[z, pl.ds(half * 16, 16)], x.at[z + 2, rows, ch, :], x_send.at[z, i], x_recv.at[z, i], s, chan
        )

    def give(z):
        vol_copy[1, z].wait()
        given[z] = jnp.swapaxes(landed[1, z], 0, 1)
        x_copy(z, 1).start()
        x_copy(z, 2).start()
        vol_copy[0, z].wait()
        final[0] = jnp.swapaxes(landed[0, z], 0, 1)
        x[z + 2, 2:18, ch, :] = final[0, pl.ds(core * 16, 16)]
        shared[z] = final[0, pl.ds(other * 16, 16)]
        x_copy(z, 0).start()

    def z_copy(z, part):
        lands, slab = {0: (6, down), 1: (7, down), 2: (0, up), 3: (1, up)}[z]
        channels = (near_ch, far_ch)[part]
        return remote(
            x.at[z + 2, pl.ds(2, 16), channels, :], x.at[lands, pl.ds(2, 16), channels, :],
            z_send.at[z, part], z_recv.at[z, part], slab, across,
        )

    def send_z(z, part):
        @pl.when(has_down if z < 2 else has_up)
        def _():
            z_copy(z, part).start()

    def t_copy(layer):
        return remote(
            x.at[layer, pl.ds(16 - 14 * core, 2)], x.at[layer, pl.ds(18 * core, 2)],
            t_send.at[layer], t_recv.at[layer], s, sib,
        )

    for z in LAYERS:
        give(z)
        if z == 0:
            start_w(0)
            start_w(1)
    start_w(2)
    for z in LAYERS:
        x_copy(z, 0).wait_recv()
        if z < 2:
            send_z(z, 0)
        if z == 0:
            pass_w(0)
            pass_w(1)
        x_copy(z, 1).wait_recv()
        x_copy(z, 2).wait_recv()
        if z < 2:
            send_z(z, 1)
        t_copy(z + 2).start()
    for z in (3, 2):
        send_z(z, 0)
        send_z(z, 1)
    pass_w(2)
    for n in range(3):
        end_w(n)

    def turn(i, carry):
        w2t[i] = w2[i].T
        return carry

    lax.fori_loop(0, 27, turn, 0)

    def outer(z, has):
        lands = {0: 6, 1: 7, 2: 0, 3: 1}[z]

        @pl.when(has)
        def _():
            for part in range(2):
                z_copy(z, part).wait_recv()
            t_copy(lands).start()
            t_copy(lands).wait_recv()

    def o_copy(z, i):
        chan = (sib, across, diag)[i]
        theirs_ch = pl.ds(pl.multiple_of(chan * 32, 32), 32)
        return remote(
            res.at[z, :, theirs_ch, :], back.at[mine, z, pl.ds(core * 16, 16)],
            o_send.at[z, i], o_recv.at[z, i], s, chan,
        )

    def o_own(z):
        return pltpu.make_async_copy(res.at[z, :, ch, :], back.at[mine, z, pl.ds(core * 16, 16)], o_self.at[z])

    def step(j, carry):
        layer = jnp.where(j < 4, j + 2, 5 - j)
        z_out = jnp.where(j < 4, j, 5 - j)

        @pl.when(j == 0)
        def _():
            for i in range(2, 5):
                t_copy(i).wait_recv()

        @pl.when(j == 1)
        def _():
            t_copy(5).wait_recv()

        for step_at, z, has in ((2, 0, has_up), (3, 1, has_up), (4, 3, has_down), (5, 2, has_down)):

            @pl.when(j == step_at)
            def _():
                outer(z, has)

        inside = jnp.logical_and(jnp.logical_or(has_up, j != 3), jnp.logical_or(has_down, j != 5))

        @pl.when(inside)
        def _():
            weights = stacked(w1)
            b = bias[0]
            for row in range(0, 18, 2):
                hid[layer, row], hid[layer, row + 1] = conv_rows(x, layer, row, weights, b)
            hid[layer, 17 * core] = jnp.zeros((128, 128), BF16)

        @pl.when(j >= 2)
        def _():
            weights = stacked(w2t)
            b = bias[1]
            for row in range(0, 16, 2):
                res[z_out, row], res[z_out, row + 1] = conv_rows(hid, z_out, row, weights, b)
            for i in (1, 2, 0):
                o_copy(z_out, i).start()
            o_own(z_out).start()

        return carry

    lax.fori_loop(0, 6, step, 0)

    def out_copy(b, z):
        return pltpu.make_async_copy(final.at[b * 4 + z], out.at[b, z], sem_out.at[b, z])

    for z in (2, 3, 1, 0):
        o_own(z).wait()
        for i in range(3):
            o_copy(z, i).wait_recv()
        for b in range(2):
            final[b * 4 + z] = jnp.swapaxes(back[b, z], 0, 1)
            out_copy(b, z).start()

    for n in range(3):
        for i, chan_from, slab, chan in ((0, k, s, sib), (1, k, pair, across), (2, across, s, sib)):
            w_copy(n, i, chan_from, slab, chan).wait_send()
    for z in LAYERS:
        for i in range(3):
            x_copy(z, i).wait_send()
            o_copy(z, i).wait_send()
        t_copy(z + 2).wait_send()

        @pl.when(has_down if z < 2 else has_up)
        def _():
            z_copy(z, 0).wait_send()
            z_copy(z, 1).wait_send()

        @pl.when(has_up if z < 2 else has_down)
        def _():
            t_copy({0: 6, 1: 7, 2: 0, 3: 1}[z]).wait_send()

        for b in range(2):
            out_copy(b, z).wait()


def body(volume, first_kernel, first_bias, second_kernel, second_bias):
    w1 = jnp.transpose(first_kernel, (0, 1, 2, 4, 3)).reshape(27, 32, 128)
    w2 = second_kernel.reshape(27, 32, 128)
    bias = jnp.broadcast_to(jnp.stack([first_bias, second_bias])[:, :, None], (2, 32, 128))
    hbm = pl.BlockSpec(memory_space=pl.ANY)
    dma = pltpu.SemaphoreType.DMA
    return pl.pallas_call(
        kernel,
        out_shape=jax.ShapeDtypeStruct((2, 4, 32, 32, 128), BF16),
        in_specs=[hbm] * 4,
        out_specs=hbm,
        scratch_shapes=[
            pltpu.VMEM((2, 4, 32, 32, 128), BF16),
            pltpu.VMEM((4, 32, 32, 128), BF16),
            pltpu.VMEM((4, 16, 32, 128), BF16),
            pltpu.VMEM((8, 20, 128, 128), BF16),
            pltpu.VMEM((6, 18, 128, 128), BF16),
            pltpu.VMEM((4, 16, 128, 128), BF16),
            pltpu.VMEM((2, 4, 32, 32, 128), BF16),
            pltpu.VMEM((8, 32, 32, 128), BF16),
            pltpu.VMEM((27, 128, 128), BF16),
            pltpu.VMEM((27, 128, 128), BF16),
            pltpu.VMEM((27, 128, 128), BF16),
            pltpu.VMEM((2, 128, 128), F32),
            dma((2, 4)),
            dma((3,)),
            dma((3, 3)),
            dma((3, 3)),
            dma((4, 3)),
            dma((4, 3)),
            dma((8,)),
            dma((8,)),
            dma((4, 2)),
            dma((4, 2)),
            dma((4, 3)),
            dma((4, 3)),
            dma((4,)),
            dma((2, 4)),
        ],
        name="two_convolutions",
        cost_estimate=pl.CostEstimate(flops=20_000_000_000, bytes_accessed=8_000_000, transcendentals=0),
        compiler_params=pltpu.CompilerParams(
            collective_id=0, has_side_effects=True, vmem_limit_bytes=48 * 1024 * 1024
        ),
    )(volume, w1, w2, bias)


def solution(mesh):
    return jax.shard_map(
        body,
        mesh=mesh,
        in_specs=(
            P(None, "slab", "chan", None, None),
            P(None, None, None, None, "chan"),
            P("chan"),
            P(None, None, None, "chan", None),
            P("chan"),
        ),
        out_specs=P(None, "slab", "chan", None, None),
        check_vma=False,
    )
```

```python
import jax
import jax.numpy as jnp
from jax import lax
from jax.experimental import pallas as pl
from jax.experimental.pallas import tpu as pltpu
from jax.sharding import PartitionSpec as P

MESH = pl.DeviceIdType.MESH
SLABS = 32
BF16 = jnp.bfloat16
F32 = jnp.float32
CHUNKS = ((0, 6), (6, 4), (10, 4), (14, 2))
HIDDEN = (
    ((0, 6), (6, 4), (10, 4), (14, 3)),
    ((0, 4), (4, 2), (6, 2), (8, 2), (10, 2), (12, 2), (14, 2), (16, 1)),
)


def conv_rows(source, layer, row, weights, bias):
    taps = [
        jnp.concatenate([source[layer + a, row + c], source[layer + a, row + c + 1]], axis=1)
        for a in range(3)
        for c in range(3)
    ]
    sums = jnp.dot(weights, jnp.concatenate(taps, axis=0), preferred_element_type=F32)
    lane = lax.broadcasted_iota(jnp.int32, (128, 128), 1)
    outs = []
    for r in range(2):
        cols = slice(128 * r, 128 * r + 128)
        left = jnp.where(lane == 0, 0.0, pltpu.roll(sums[0:128, cols], 1, 1))
        right = jnp.where(lane == 127, 0.0, pltpu.roll(sums[256:384, cols], 127, 1))
        outs.append(jnp.maximum(sums[128:256, cols] + left + right + bias, 0.0).astype(BF16))
    return outs


def stacked(taps, core):
    parts = []
    for a in range(3):
        for c in range(3):
            at = 9 * a + 3 * (c + (1 - core) * (2 - 2 * c))
            parts.append(taps[pl.ds(at, 3)].reshape(384, 128))
    return jnp.concatenate(parts, axis=1)


def halves(rows):
    return jnp.stack([rows[15 - d] for d in range(16)]), rows[16:]


def kernel(
    vol, w1_in, w2_in, b1_in, b2_in, out,
    landed, given, own, x, hid, res, back, final, w, w2t, rows8, bias, b1_s, b2_s, sem_b,
    sem_vol, sem_w, w_send, w_recv, b_send, b_recv, x_send, x_recv, s_send, s_recv, t_send, t_recv,
    near_send, near_recv, far_send, far_recv, h_send, h_recv,
    in_send, in_recv, out_send, out_recv, sem_out,
):
    s = lax.axis_index("slab")
    k = lax.axis_index("chan")
    core = lax.rem(k, 2)
    chip = k // 2
    other = 1 - core
    sib = 2 * chip + other
    across = 2 * (1 - chip) + core
    diag = 2 * (1 - chip) + other
    mine = lax.rem(chip + s, 2)
    theirs = 1 - mine
    up, down = lax.rem(s + 1, SLABS), lax.rem(s + SLABS - 1, SLABS)
    y = lax.rem(s // 2, 4)
    odd = lax.rem(s // 8, 2)
    twin = 8 * (1 - 2 * odd)
    pair = s + 1 - 2 * lax.rem(s, 2)
    has_down, has_up = s > 0, s < SLABS - 1

    def y_peer(m):
        return s + 2 * (lax.rem(y + m, 4) - y)

    def chans(chan):
        return pl.ds(pl.multiple_of(chan * 32, 32), 32)

    ch = chans(k)
    far_ch = pl.ds(pl.multiple_of((1 - chip) * 64, 64), 64)

    def remote(src, dst, send, recv, slab, chan):
        return pltpu.make_async_remote_copy(
            src_ref=src, dst_ref=dst, send_sem=send, recv_sem=recv, device_id=(slab, chan), device_id_type=MESH
        )

    w[27] = jnp.zeros((128, 128), BF16)
    w[55] = jnp.zeros((128, 128), BF16)
    barrier = pltpu.get_barrier_semaphore()
    peers = [(s, sib), (s, across), (s, diag), (up, across), (down, across), (up, diag), (down, diag)]
    peers += [(y_peer(m), k) for m in (1, 2, 3)] + [(y_peer(m) + twin, k) for m in range(4)]
    for slab, chan in peers:
        pl.semaphore_signal(barrier, inc=1, device_id=(slab, chan), device_id_type=MESH)

    def own_w(n):
        return pltpu.make_async_copy((w1_in, w2_in)[n], w.at[pl.ds(28 * n, 27), ch, :], sem_w.at[n])

    def b_load(n):
        return pltpu.make_async_copy((b1_in, b2_in)[n], (b1_s, b2_s)[n], sem_b.at[n])

    def vol_copy(which, z):
        return pltpu.make_async_copy(vol.at[(mine, theirs)[which], z], landed.at[which, z], sem_vol.at[which, z])

    for n in range(2):
        b_load(n).start()
        own_w(n).start()
    for which, z in ((1, 0), (1, 1), (1, 2), (1, 3), (0, 0), (0, 3), (0, 1), (0, 2)):
        vol_copy(which, z).start()

    def blank():
        def blank_rows(i, carry):
            x[i, 18:20] = jnp.zeros((2, 128, 128), BF16)
            hid[i, 17] = jnp.zeros((128, 128), BF16)
            return carry

        lax.fori_loop(0, 6, blank_rows, 0)

        def blank_layer(layer):
            def row(i, carry):
                x[layer, i] = jnp.zeros((128, 128), BF16)
                hid[layer, i] = jnp.zeros((128, 128), BF16)
                return carry

            lax.fori_loop(0, 18, row, 0)

        @pl.when(jnp.logical_not(has_down))
        def _():
            blank_layer(0)

        @pl.when(jnp.logical_not(has_up))
        def _():
            blank_layer(5)

    at_row = lax.broadcasted_iota(jnp.int32, (8, 128), 0)
    at_lane = lax.broadcasted_iota(jnp.int32, (8, 128), 1) - 32 * k
    for n in range(2):
        b_load(n).wait()
    tile = jnp.zeros((8, 128), F32)
    for i in range(32):
        value = jnp.where(at_row == 0, b1_s[i], b2_s[i])
        tile = jnp.where(jnp.logical_and(at_lane == i, at_row < 2), value, tile)
    rows8[k] = tile

    def keep(which, z):
        vol_copy(which, z).wait()
        to = (own, given)[which]
        to[0, z], to[1, z] = halves(jnp.swapaxes(landed[which, z], 0, 1))

    for which, z in ((1, 0), (1, 1), (1, 2), (1, 3), (0, 0), (0, 3)):
        keep(which, z)
    pl.semaphore_wait(barrier, len(peers))

    def w_part(n, chan_from, quarter=None):
        taps = pl.ds(28 * n, 28) if quarter is None else pl.ds(28 * n + 7 * quarter, 7)
        return w.at[taps, chans(chan_from), :]

    def w_copy(i, receives=False):
        if i < 2:
            part, slab, chan = w_part(i, sib if receives else k), s, sib
        elif i < 4:
            part, slab, chan = w_part(i - 2, diag if receives else across), s, sib
        elif i == 4:
            part, slab, chan = w_part(odd, across if receives else k, y), pair, across
        else:
            m = i - 4 if i < 8 else i - 8
            n = odd if i < 8 or not receives else 1 - odd
            slab = y_peer(m) if i < 8 else y_peer(m) + twin
            part, chan = w_part(n, across, lax.rem(y + 4 - m, 4) if receives else y), k
        return remote(part, part, w_send.at[i], w_recv.at[i], slab, chan)

    def b_copy(i, receives=False):
        chan = (sib, across, diag)[i]
        part = rows8.at[chan if receives else k]
        return remote(part, part, b_send.at[i], b_recv.at[i], s, chan)

    for i in range(3):
        b_copy(i).start()
    for n in range(2):
        own_w(n).wait()
    w_copy(4).start()

    def x_copy(q, i):
        row, rows = CHUNKS[q]
        half, chan = ((core, across), (other, diag))[i]
        return remote(
            given.at[half, :, pl.ds(row, rows)], x.at[pl.ds(1, 4), pl.ds(row + 2, rows), ch, :],
            x_send.at[q, i], x_recv.at[q, i], s, chan,
        )

    def s_copy():
        return remote(own.at[other], x.at[pl.ds(1, 4), pl.ds(2, 16), ch, :], s_send, s_recv, s, sib)

    ENDS = ((3, 0, up, has_up, has_down), (0, 5, down, has_down, has_up))

    def near_copy(way, i):
        z, lands, slab = ENDS[way][:3]
        half, chan = ((core, across), (other, diag))[i]
        return remote(
            own.at[half, z], x.at[lands, pl.ds(2, 16), ch, :], near_send.at[way, i], near_recv.at[way, i], slab, chan
        )

    def far_copy(way, q):
        z, lands, slab = ENDS[way][:3]
        row, rows = CHUNKS[q]
        return remote(
            x.at[z + 1, pl.ds(row + 2, rows), far_ch, :], x.at[lands, pl.ds(row + 2, rows), far_ch, :],
            far_send.at[way, q], far_recv.at[way, q], slab, across,
        )

    def h_copy(way, q):
        z, lands, slab = ENDS[way][:3]
        rows = pl.ds(*HIDDEN[way][q])
        return remote(hid.at[z + 1, rows], hid.at[lands, rows], h_send.at[way, q], h_recv.at[way, q], slab, across)

    def t_copy(group, i):
        layers = (pl.ds(1, 4), 0, 5)[group]
        return remote(x.at[layers, 2 + i], x.at[layers, 1 - i], t_send.at[group, i], t_recv.at[group, i], s, sib)

    def start_ways(copy, way, *at):
        @pl.when(ENDS[way][3])
        def _():
            copy(way, *at).start()

    for q in range(4):
        for i in range(2):
            x_copy(q, i).start()
    for way in (1, 0):
        for i in range(2):
            start_ways(near_copy, way, i)
    for n in range(2):
        w_copy(n).start()
    for z in (1, 2):
        keep(0, z)
    s_copy().start()
    for z in range(4):
        x[z + 1, 2:18, ch, :] = own[core, z]
    blank()

    w_copy(4, True).wait_recv()
    for i in range(5, 12):
        w_copy(i).start()
    for i in range(3):
        b_copy(i, True).wait_recv()
    both = rows8[0] + rows8[1] + rows8[2] + rows8[3]
    for n in range(2):
        bias[n] = jnp.broadcast_to(both[n : n + 1], (128, 128)).T
    for i in range(5, 12):
        w_copy(i, True).wait_recv()
    for n in range(2):
        w_copy(n + 2).start()

    def turn(i, carry):
        w2t[i] = w[28 + i].T
        return carry

    s_copy().wait_recv()

    def o_copy(inner, z, q, i):
        chan = (sib, across, diag)[i]
        if inner:
            z, rows = pl.ds(1, 2), pl.ds(pl.multiple_of(4 * q, 4), 4)
            sems = in_send.at[q, i], in_recv.at[q, i]
        else:
            rows = pl.ds(pl.multiple_of(2 * q, 2), 2)
            sems = out_send.at[z // 3, q, i], out_recv.at[z // 3, q, i]
        return remote(res.at[z, rows, chans(chan), :], back.at[mine, z, core, rows], *sems, s, chan)

    def first(layers, row):
        weights, b = stacked(w, core), bias[0]
        for z in layers:
            for r in row:
                hid[z + 1, r], hid[z + 1, r + 1] = conv_rows(x, z, r, weights, b)

    def second(layers, row):
        weights, b = stacked(w2t, core), bias[1]
        for z in layers:
            for r in row:
                res[z, r], res[z, r + 1] = conv_rows(hid, z, r, weights, b)

    def last_row(layers):
        for z in layers:
            hid[z + 1, 17] = jnp.zeros((128, 128), BF16)

    def step(j, carry):
        @pl.when(j < 4)
        def _():
            for q in range(4):

                @pl.when(j == q)
                def _():
                    for i in range(2):
                        x_copy(q, i).wait_recv()
                    for way in (1, 0):
                        start_ways(far_copy, way, q)
                    if q == 0:
                        for i in range(2):
                            t_copy(0, i).start()
                        for n in (0, 2):
                            w_copy(n, True).wait_recv()

            first((1, 2), (4 * j + 2, 4 * j + 4))

            @pl.when(j == 0)
            def _():
                for i in range(2):
                    t_copy(0, i).wait_recv()
                first((1, 2), (0,))
                for n in (1, 3):
                    w_copy(n, True).wait_recv()
                lax.fori_loop(0, 27, turn, 0)

            @pl.when(j == 3)
            def _():
                last_row((1, 2))

        @pl.when(j >= 1)
        def _():
            i = j - 1
            for q in range(4):

                @pl.when(i == q)
                def _():
                    for way in (1, 0):

                        @pl.when(ENDS[way][4])
                        def _():
                            if q == 0:
                                for n in range(2):
                                    near_copy(way, n).wait_recv()
                            far_copy(way, q).wait_recv()
                            if q == 0:
                                for n in range(2):
                                    t_copy(1 + way, n).start()

            first((3, 0), (4 * i + 2, 4 * i + 4))

            @pl.when(i == 0)
            def _():
                for way in (1, 0):

                    @pl.when(ENDS[way][4])
                    def _():
                        for n in range(2):
                            t_copy(1 + way, n).wait_recv()

                first((3, 0), (0,))

            @pl.when(i == 3)
            def _():
                last_row((3, 0))

            for q in range(4):

                @pl.when(i == q)
                def _():
                    start_ways(h_copy, 0, q)
                    if q == 3:
                        for n in range(8):
                            start_ways(h_copy, 1, n)

            second((1, 2), (4 * i, 4 * i + 2))
            for n in (1, 2, 0):
                o_copy(True, None, i, n).start()

        return carry

    lax.fori_loop(0, 5, step, 0)

    def out_copy(b, z):
        return pltpu.make_async_copy(final.at[b * 4 + z], out.at[b, z], sem_out.at[b, z])

    def finish(z):
        back[mine, z, core] = res[z, :, ch, :]
        for b in range(2):
            rows = [back[b, z, 0, 15 - d] for d in range(16)] + [back[b, z, 1, d] for d in range(16)]
            final[b * 4 + z] = jnp.swapaxes(jnp.stack(rows), 0, 1)
            out_copy(b, z).start()

    def last_step(j, carry):
        z = 3 * (j // 8)
        i = lax.rem(j, 8)
        for way in range(2):
            for q in range((4, 8)[way]):

                @pl.when(jnp.logical_and(j == (2 * q, 8 + q)[way], ENDS[way][4]))
                def _():
                    h_copy(way, q).wait_recv()

        second((z,), (2 * i,))
        for n in (1, 2, 0):
            o_copy(False, z, i, n).start()

        @pl.when(j == 7)
        def _():
            for q in range(4):
                for n in range(3):
                    o_copy(True, None, q, n).wait_recv()
            finish(1)
            finish(2)

        @pl.when(j == 13)
        def _():
            for q in range(8):
                for n in range(3):
                    o_copy(False, 0, q, n).wait_recv()
            finish(0)

        return carry

    lax.fori_loop(0, 16, last_step, 0)
    for q in range(8):
        for n in range(3):
            o_copy(False, 3, q, n).wait_recv()
    finish(3)

    for i in range(12):
        w_copy(i).wait_send()
    for i in range(3):
        b_copy(i).wait_send()
    s_copy().wait_send()
    for i in range(2):
        t_copy(0, i).wait_send()
    for way in range(2):

        @pl.when(ENDS[way][3])
        def _():
            for i in range(2):
                near_copy(way, i).wait_send()
            for q in range(4):
                far_copy(way, q).wait_send()
            for q in range((4, 8)[way]):
                h_copy(way, q).wait_send()

        @pl.when(ENDS[way][4])
        def _():
            for i in range(2):
                t_copy(1 + way, i).wait_send()

    for q in range(4):
        for i in range(2):
            x_copy(q, i).wait_send()
        for i in range(3):
            o_copy(True, None, q, i).wait_send()
    for q in range(8):
        for i in range(3):
            o_copy(False, 0, q, i).wait_send()
            o_copy(False, 3, q, i).wait_send()
    for z in range(4):
        for b in range(2):
            out_copy(b, z).wait()


def body(volume, first_kernel, first_bias, second_kernel, second_bias):
    w1 = jnp.transpose(first_kernel, (0, 1, 2, 4, 3)).reshape(27, 32, 128)
    w2 = second_kernel.reshape(27, 32, 128)
    dma = pltpu.SemaphoreType.DMA
    return pl.pallas_call(
        kernel,
        out_shape=jax.ShapeDtypeStruct((2, 4, 32, 32, 128), BF16),
        in_specs=[pl.BlockSpec(memory_space=pl.ANY)] * 3 + [pl.BlockSpec(memory_space=pl.ANY)] * 2,
        out_specs=pl.BlockSpec(memory_space=pl.ANY),
        scratch_shapes=[
            pltpu.VMEM((2, 4, 32, 32, 128), BF16),
            pltpu.VMEM((2, 4, 16, 32, 128), BF16),
            pltpu.VMEM((2, 4, 16, 32, 128), BF16),
            pltpu.VMEM((6, 20, 128, 128), BF16),
            pltpu.VMEM((6, 18, 128, 128), BF16),
            pltpu.VMEM((4, 16, 128, 128), BF16),
            pltpu.VMEM((2, 4, 2, 16, 32, 128), BF16),
            pltpu.VMEM((8, 32, 32, 128), BF16),
            pltpu.VMEM((56, 128, 128), BF16),
            pltpu.VMEM((27, 128, 128), BF16),
            pltpu.VMEM((4, 8, 128), F32),
            pltpu.VMEM((2, 128, 128), F32),
            pltpu.SMEM((32,), F32),
            pltpu.SMEM((32,), F32),
            dma((2,)),
            dma((2, 4)),
            dma((2,)),
            dma((12,)),
            dma((12,)),
            dma((3,)),
            dma((3,)),
            dma((4, 2)),
            dma((4, 2)),
            dma,
            dma,
            dma((3, 2)),
            dma((3, 2)),
            dma((2, 2)),
            dma((2, 2)),
            dma((2, 4)),
            dma((2, 4)),
            dma((2, 8)),
            dma((2, 8)),
            dma((4, 3)),
            dma((4, 3)),
            dma((2, 8, 3)),
            dma((2, 8, 3)),
            dma((2, 4)),
        ],
        name="two_convolutions",
        cost_estimate=pl.CostEstimate(flops=20_000_000_000, bytes_accessed=8_000_000, transcendentals=0),
        compiler_params=pltpu.CompilerParams(
            collective_id=0, has_side_effects=True, vmem_limit_bytes=60 * 1024 * 1024
        ),
    )(volume, w1, w2, first_bias, second_bias)


def solution(mesh):
    return jax.shard_map(
        body,
        mesh=mesh,
        in_specs=(
            P(None, "slab", "chan", None, None),
            P(None, None, None, None, "chan"),
            P("chan"),
            P(None, None, None, "chan", None),
            P("chan"),
        ),
        out_specs=P(None, "slab", "chan", None, None),
        check_vma=False,
    )
```

```python
import jax
import jax.numpy as jnp
from jax import lax
from jax.experimental import pallas as pl
from jax.experimental.pallas import tpu as pltpu
from jax.sharding import PartitionSpec as P

MESH = pl.DeviceIdType.MESH
SLABS = 32
BF16 = jnp.bfloat16
F32 = jnp.float32
CHUNKS = ((0, 6), (6, 4), (10, 4), (14, 2))
HIDDEN = (
    ((0, 6), (6, 4), (10, 4), (14, 3)),
    ((0, 4), (4, 2), (6, 2), (8, 2), (10, 2), (12, 2), (14, 2), (16, 1)),
)


def conv_rows(source, layer, row, weights, bias):
    taps = [
        jnp.concatenate([source[layer + a, row + c], source[layer + a, row + c + 1]], axis=1)
        for a in range(3)
        for c in range(3)
    ]
    sums = jnp.dot(weights, jnp.concatenate(taps, axis=0), preferred_element_type=F32)
    lane = lax.broadcasted_iota(jnp.int32, (128, 128), 1)
    outs = []
    for r in range(2):
        cols = slice(128 * r, 128 * r + 128)
        left = jnp.where(lane == 0, 0.0, pltpu.roll(sums[0:128, cols], 1, 1))
        right = jnp.where(lane == 127, 0.0, pltpu.roll(sums[256:384, cols], 127, 1))
        outs.append(jnp.maximum(sums[128:256, cols] + left + right + bias, 0.0).astype(BF16))
    return outs


def stacked(taps, core):
    parts = []
    for a in range(3):
        for c in range(3):
            at = 9 * a + 3 * (c + (1 - core) * (2 - 2 * c))
            parts.append(taps[pl.ds(at, 3)].reshape(384, 128))
    return jnp.concatenate(parts, axis=1)


def halves(rows):
    return jnp.stack([rows[15 - d] for d in range(16)]), rows[16:]


def kernel(
    vol, w1_in, w2_in, b1_in, b2_in, back,
    landed, given, own, x, hid, res, w, w2t, rows8, bias, b1_s, b2_s, sem_b,
    sem_vol, sem_w, w_send, w_recv, b_send, b_recv, x_send, x_recv, s_send, s_recv, t_send, t_recv,
    near_send, near_recv, far_send, far_recv, h_send, h_recv,
    in_send, in_recv, out_send, out_recv, sem_out,
):
    s = lax.axis_index("slab")
    k = lax.axis_index("chan")
    core = lax.rem(k, 2)
    chip = k // 2
    other = 1 - core
    sib = 2 * chip + other
    across = 2 * (1 - chip) + core
    diag = 2 * (1 - chip) + other
    mine = lax.rem(chip + s, 2)
    theirs = 1 - mine
    up, down = lax.rem(s + 1, SLABS), lax.rem(s + SLABS - 1, SLABS)
    y = lax.rem(s // 2, 4)
    odd = lax.rem(s // 8, 2)
    twin = 8 * (1 - 2 * odd)
    pair = s + 1 - 2 * lax.rem(s, 2)
    has_down, has_up = s > 0, s < SLABS - 1

    def y_peer(m):
        return s + 2 * (lax.rem(y + m, 4) - y)

    def chans(chan):
        return pl.ds(pl.multiple_of(chan * 32, 32), 32)

    ch = chans(k)
    far_ch = pl.ds(pl.multiple_of((1 - chip) * 64, 64), 64)

    def remote(src, dst, send, recv, slab, chan):
        return pltpu.make_async_remote_copy(
            src_ref=src, dst_ref=dst, send_sem=send, recv_sem=recv, device_id=(slab, chan), device_id_type=MESH
        )

    w[27] = jnp.zeros((128, 128), BF16)
    w[55] = jnp.zeros((128, 128), BF16)
    barrier = pltpu.get_barrier_semaphore()
    peers = [(s, sib), (s, across), (s, diag), (up, across), (down, across), (up, diag), (down, diag)]
    peers += [(y_peer(m), k) for m in (1, 2, 3)] + [(y_peer(m) + twin, k) for m in range(4)]
    for slab, chan in peers:
        pl.semaphore_signal(barrier, inc=1, device_id=(slab, chan), device_id_type=MESH)

    def own_w(n):
        return pltpu.make_async_copy((w1_in, w2_in)[n], w.at[pl.ds(28 * n, 27), ch, :], sem_w.at[n])

    def b_load(n):
        return pltpu.make_async_copy((b1_in, b2_in)[n], (b1_s, b2_s)[n], sem_b.at[n])

    def vol_copy(which, z):
        return pltpu.make_async_copy(vol.at[(mine, theirs)[which], z], landed.at[which, z], sem_vol.at[which, z])

    for n in range(2):
        b_load(n).start()
        own_w(n).start()
    for which, z in ((1, 0), (1, 1), (1, 2), (1, 3), (0, 0), (0, 3), (0, 1), (0, 2)):
        vol_copy(which, z).start()

    def blank():
        def blank_rows(i, carry):
            x[i, 18:20] = jnp.zeros((2, 128, 128), BF16)
            hid[i, 17] = jnp.zeros((128, 128), BF16)
            return carry

        lax.fori_loop(0, 6, blank_rows, 0)

        def blank_layer(layer):
            def row(i, carry):
                x[layer, i] = jnp.zeros((128, 128), BF16)
                hid[layer, i] = jnp.zeros((128, 128), BF16)
                return carry

            lax.fori_loop(0, 18, row, 0)

        @pl.when(jnp.logical_not(has_down))
        def _():
            blank_layer(0)

        @pl.when(jnp.logical_not(has_up))
        def _():
            blank_layer(5)

    at_row = lax.broadcasted_iota(jnp.int32, (8, 128), 0)
    at_lane = lax.broadcasted_iota(jnp.int32, (8, 128), 1) - 32 * k
    for n in range(2):
        b_load(n).wait()
    tile = jnp.zeros((8, 128), F32)
    for i in range(32):
        value = jnp.where(at_row == 0, b1_s[i], b2_s[i])
        tile = jnp.where(jnp.logical_and(at_lane == i, at_row < 2), value, tile)
    rows8[k] = tile

    def keep(which, z):
        vol_copy(which, z).wait()
        to = (own, given)[which]
        to[0, z], to[1, z] = halves(jnp.swapaxes(landed[which, z], 0, 1))

    for which, z in ((1, 0), (1, 1), (1, 2), (1, 3), (0, 0), (0, 3)):
        keep(which, z)
    pl.semaphore_wait(barrier, len(peers))

    def w_part(n, chan_from, quarter=None):
        taps = pl.ds(28 * n, 28) if quarter is None else pl.ds(28 * n + 7 * quarter, 7)
        return w.at[taps, chans(chan_from), :]

    def w_copy(i, receives=False):
        if i < 2:
            part, slab, chan = w_part(i, sib if receives else k), s, sib
        elif i < 4:
            part, slab, chan = w_part(i - 2, diag if receives else across), s, sib
        elif i == 4:
            part, slab, chan = w_part(odd, across if receives else k, y), pair, across
        else:
            m = i - 4 if i < 8 else i - 8
            n = odd if i < 8 or not receives else 1 - odd
            slab = y_peer(m) if i < 8 else y_peer(m) + twin
            part, chan = w_part(n, across, lax.rem(y + 4 - m, 4) if receives else y), k
        return remote(part, part, w_send.at[i], w_recv.at[i], slab, chan)

    def b_copy(i, receives=False):
        chan = (sib, across, diag)[i]
        part = rows8.at[chan if receives else k]
        return remote(part, part, b_send.at[i], b_recv.at[i], s, chan)

    for i in range(3):
        b_copy(i).start()
    for n in range(2):
        own_w(n).wait()
    w_copy(4).start()

    def x_copy(q, i):
        row, rows = CHUNKS[q]
        half, chan = ((core, across), (other, diag))[i]
        return remote(
            given.at[half, :, pl.ds(row, rows)], x.at[pl.ds(1, 4), pl.ds(row + 2, rows), ch, :],
            x_send.at[q, i], x_recv.at[q, i], s, chan,
        )

    def s_copy():
        return remote(own.at[other], x.at[pl.ds(1, 4), pl.ds(2, 16), ch, :], s_send, s_recv, s, sib)

    ENDS = ((3, 0, up, has_up, has_down), (0, 5, down, has_down, has_up))

    def near_copy(way, i):
        z, lands, slab = ENDS[way][:3]
        half, chan = ((core, across), (other, diag))[i]
        return remote(
            own.at[half, z], x.at[lands, pl.ds(2, 16), ch, :], near_send.at[way, i], near_recv.at[way, i], slab, chan
        )

    def far_copy(way, q):
        z, lands, slab = ENDS[way][:3]
        row, rows = CHUNKS[q]
        return remote(
            x.at[z + 1, pl.ds(row + 2, rows), far_ch, :], x.at[lands, pl.ds(row + 2, rows), far_ch, :],
            far_send.at[way, q], far_recv.at[way, q], slab, across,
        )

    def h_copy(way, q):
        z, lands, slab = ENDS[way][:3]
        rows = pl.ds(*HIDDEN[way][q])
        return remote(hid.at[z + 1, rows], hid.at[lands, rows], h_send.at[way, q], h_recv.at[way, q], slab, across)

    def t_copy(group, i):
        layers = (pl.ds(1, 4), 0, 5)[group]
        return remote(x.at[layers, 2 + i], x.at[layers, 1 - i], t_send.at[group, i], t_recv.at[group, i], s, sib)

    def start_ways(copy, way, *at):
        @pl.when(ENDS[way][3])
        def _():
            copy(way, *at).start()

    for q in range(4):
        for i in range(2):
            x_copy(q, i).start()
    for way in (1, 0):
        for i in range(2):
            start_ways(near_copy, way, i)
    for n in range(2):
        w_copy(n).start()
    for z in (1, 2):
        keep(0, z)
    s_copy().start()
    for z in range(4):
        x[z + 1, 2:18, ch, :] = own[core, z]
    blank()

    w_copy(4, True).wait_recv()
    for i in range(5, 12):
        w_copy(i).start()
    for i in range(3):
        b_copy(i, True).wait_recv()
    both = rows8[0] + rows8[1] + rows8[2] + rows8[3]
    for n in range(2):
        bias[n] = jnp.broadcast_to(both[n : n + 1], (128, 128)).T
    for i in range(5, 12):
        w_copy(i, True).wait_recv()
    for n in range(2):
        w_copy(n + 2).start()

    def turn(i, carry):
        w2t[i] = w[28 + i].T
        return carry

    s_copy().wait_recv()

    def o_copy(inner, z, q, i):
        chan = (sib, across, diag)[i]
        if inner:
            z, rows = pl.ds(1, 2), pl.ds(pl.multiple_of(4 * q, 4), 4)
            sems = in_send.at[q, i], in_recv.at[q, i]
        else:
            rows = pl.ds(pl.multiple_of(2 * q, 2), 2)
            sems = out_send.at[z // 3, q, i], out_recv.at[z // 3, q, i]
        return remote(res.at[z, rows, chans(chan), :], back.at[mine, z, core, rows], *sems, s, chan)

    def first(layers, row):
        weights, b = stacked(w, core), bias[0]
        for z in layers:
            for r in row:
                hid[z + 1, r], hid[z + 1, r + 1] = conv_rows(x, z, r, weights, b)

    def second(layers, row):
        weights, b = stacked(w2t, core), bias[1]
        for z in layers:
            for r in row:
                res[z, r], res[z, r + 1] = conv_rows(hid, z, r, weights, b)

    def last_row(layers):
        for z in layers:
            hid[z + 1, 17] = jnp.zeros((128, 128), BF16)

    def step(j, carry):
        @pl.when(j < 4)
        def _():
            for q in range(4):

                @pl.when(j == q)
                def _():
                    for i in range(2):
                        x_copy(q, i).wait_recv()
                    for way in (1, 0):
                        start_ways(far_copy, way, q)
                    if q == 0:
                        for i in range(2):
                            t_copy(0, i).start()
                        for n in (0, 2):
                            w_copy(n, True).wait_recv()

            first((1, 2), (4 * j + 2, 4 * j + 4))

            @pl.when(j == 0)
            def _():
                for i in range(2):
                    t_copy(0, i).wait_recv()
                first((1, 2), (0,))
                for n in (1, 3):
                    w_copy(n, True).wait_recv()
                lax.fori_loop(0, 27, turn, 0)

            @pl.when(j == 3)
            def _():
                last_row((1, 2))

        @pl.when(j >= 1)
        def _():
            i = j - 1
            for q in range(4):

                @pl.when(i == q)
                def _():
                    for way in (1, 0):

                        @pl.when(ENDS[way][4])
                        def _():
                            if q == 0:
                                for n in range(2):
                                    near_copy(way, n).wait_recv()
                            far_copy(way, q).wait_recv()
                            if q == 0:
                                for n in range(2):
                                    t_copy(1 + way, n).start()

            first((3, 0), (4 * i + 2, 4 * i + 4))

            @pl.when(i == 0)
            def _():
                for way in (1, 0):

                    @pl.when(ENDS[way][4])
                    def _():
                        for n in range(2):
                            t_copy(1 + way, n).wait_recv()

                first((3, 0), (0,))

            @pl.when(i == 3)
            def _():
                last_row((3, 0))

            for q in range(4):

                @pl.when(i == q)
                def _():
                    start_ways(h_copy, 0, q)
                    if q == 3:
                        for n in range(8):
                            start_ways(h_copy, 1, n)

            second((1, 2), (4 * i, 4 * i + 2))
            for n in (1, 2, 0):
                o_copy(True, None, i, n).start()

        return carry

    lax.fori_loop(0, 5, step, 0)

    def own_copy(z):
        return pltpu.make_async_copy(res.at[z, :, ch, :], back.at[mine, z, core], sem_out.at[z])

    def last_step(j, carry):
        z = 3 * (j // 8)
        i = lax.rem(j, 8)
        for way in range(2):
            for q in range((4, 8)[way]):

                @pl.when(jnp.logical_and(j == (2 * q, 8 + q)[way], ENDS[way][4]))
                def _():
                    h_copy(way, q).wait_recv()

        second((z,), (2 * i,))
        for n in (1, 2, 0):
            o_copy(False, z, i, n).start()

        @pl.when(j == 7)
        def _():
            for q in range(4):
                for n in range(3):
                    o_copy(True, None, q, n).wait_recv()
            own_copy(1).start()
            own_copy(2).start()

        @pl.when(j == 13)
        def _():
            for q in range(8):
                for n in range(3):
                    o_copy(False, 0, q, n).wait_recv()
            own_copy(0).start()

        return carry

    lax.fori_loop(0, 16, last_step, 0)
    own_copy(3).start()
    for q in range(8):
        for n in range(3):
            o_copy(False, 3, q, n).wait_recv()

    for i in range(12):
        w_copy(i).wait_send()
    for i in range(3):
        b_copy(i).wait_send()
    s_copy().wait_send()
    for i in range(2):
        t_copy(0, i).wait_send()
    for way in range(2):

        @pl.when(ENDS[way][3])
        def _():
            for i in range(2):
                near_copy(way, i).wait_send()
            for q in range(4):
                far_copy(way, q).wait_send()
            for q in range((4, 8)[way]):
                h_copy(way, q).wait_send()

        @pl.when(ENDS[way][4])
        def _():
            for i in range(2):
                t_copy(1 + way, i).wait_send()

    for q in range(4):
        for i in range(2):
            x_copy(q, i).wait_send()
        for i in range(3):
            o_copy(True, None, q, i).wait_send()
    for q in range(8):
        for i in range(3):
            o_copy(False, 0, q, i).wait_send()
            o_copy(False, 3, q, i).wait_send()
    for z in range(4):
        own_copy(z).wait()


def finish(back, out):
    for z in range(4):
        rows = [back[0, z, 0, 15 - d] for d in range(16)] + [back[0, z, 1, d] for d in range(16)]
        out[0, z] = jnp.swapaxes(jnp.stack(rows), 0, 1)


def body(volume, first_kernel, first_bias, second_kernel, second_bias):
    w1 = jnp.transpose(first_kernel, (0, 1, 2, 4, 3)).reshape(27, 32, 128)
    w2 = second_kernel.reshape(27, 32, 128)
    dma = pltpu.SemaphoreType.DMA
    back = pl.pallas_call(
        kernel,
        out_shape=jax.ShapeDtypeStruct((2, 4, 2, 16, 32, 128), BF16),
        in_specs=[pl.BlockSpec(memory_space=pl.ANY)] * 3 + [pl.BlockSpec(memory_space=pl.ANY)] * 2,
        out_specs=pl.BlockSpec(memory_space=pl.ANY),
        scratch_shapes=[
            pltpu.VMEM((2, 4, 32, 32, 128), BF16),
            pltpu.VMEM((2, 4, 16, 32, 128), BF16),
            pltpu.VMEM((2, 4, 16, 32, 128), BF16),
            pltpu.VMEM((6, 20, 128, 128), BF16),
            pltpu.VMEM((6, 18, 128, 128), BF16),
            pltpu.VMEM((4, 16, 128, 128), BF16),
            pltpu.VMEM((56, 128, 128), BF16),
            pltpu.VMEM((27, 128, 128), BF16),
            pltpu.VMEM((4, 8, 128), F32),
            pltpu.VMEM((2, 128, 128), F32),
            pltpu.SMEM((32,), F32),
            pltpu.SMEM((32,), F32),
            dma((2,)),
            dma((2, 4)),
            dma((2,)),
            dma((12,)),
            dma((12,)),
            dma((3,)),
            dma((3,)),
            dma((4, 2)),
            dma((4, 2)),
            dma,
            dma,
            dma((3, 2)),
            dma((3, 2)),
            dma((2, 2)),
            dma((2, 2)),
            dma((2, 4)),
            dma((2, 4)),
            dma((2, 8)),
            dma((2, 8)),
            dma((4, 3)),
            dma((4, 3)),
            dma((2, 8, 3)),
            dma((2, 8, 3)),
            dma((4,)),
        ],
        name="two_convolutions",
        cost_estimate=pl.CostEstimate(flops=20_000_000_000, bytes_accessed=8_000_000, transcendentals=0),
        compiler_params=pltpu.CompilerParams(
            collective_id=0, has_side_effects=True, vmem_limit_bytes=60 * 1024 * 1024
        ),
    )(volume, w1, w2, first_bias, second_bias)
    return pl.pallas_call(
        finish,
        grid=(2, 1),
        out_shape=jax.ShapeDtypeStruct((2, 4, 32, 32, 128), BF16),
        in_specs=[pl.BlockSpec((1, 4, 2, 16, 32, 128), lambda b, z: (b, z, 0, 0, 0, 0))],
        out_specs=pl.BlockSpec((1, 4, 32, 32, 128), lambda b, z: (b, z, 0, 0, 0)),
        name="rows_to_channels",
        compiler_params=pltpu.CompilerParams(vmem_limit_bytes=16 * 1024 * 1024),
    )(back)


def solution(mesh):
    return jax.shard_map(
        body,
        mesh=mesh,
        in_specs=(
            P(None, "slab", "chan", None, None),
            P(None, None, None, None, "chan"),
            P("chan"),
            P(None, None, None, "chan", None),
            P("chan"),
        ),
        out_specs=P(None, "slab", "chan", None, None),
        check_vma=False,
    )
```

```python
import jax
import jax.numpy as jnp
from jax import lax
from jax.experimental import pallas as pl
from jax.experimental.pallas import tpu as pltpu
from jax.sharding import PartitionSpec as P

MESH = pl.DeviceIdType.MESH
SLABS = 32
BF16 = jnp.bfloat16
F32 = jnp.float32
CHUNKS = ((0, 6), (6, 4), (10, 4), (14, 2))
HIDDEN = (
    ((1, 5), (6, 4), (10, 4), (14, 3)),
    ((1, 3), (4, 2), (6, 2), (8, 2), (10, 2), (12, 2), (14, 2), (16, 1)),
)


def conv_rows(source, layer, row, weights, bias):
    taps = [
        jnp.concatenate([source[layer + a, row + c], source[layer + a, row + c + 1]], axis=1)
        for a in range(3)
        for c in range(3)
    ]
    sums = jnp.dot(weights, jnp.concatenate(taps, axis=0), preferred_element_type=F32)
    lane = lax.broadcasted_iota(jnp.int32, (128, 128), 1)
    outs = []
    for r in range(2):
        cols = slice(128 * r, 128 * r + 128)
        left = jnp.where(lane == 0, 0.0, pltpu.roll(sums[0:128, cols], 1, 1))
        right = jnp.where(lane == 127, 0.0, pltpu.roll(sums[256:384, cols], 127, 1))
        outs.append(jnp.maximum(sums[128:256, cols] + left + right + bias, 0.0).astype(BF16))
    return outs


def stacked(taps, core):
    parts = []
    for a in range(3):
        for c in range(3):
            at = 9 * a + 3 * (c + (1 - core) * (2 - 2 * c))
            parts.append(taps[pl.ds(at, 3)].reshape(384, 128))
    return jnp.concatenate(parts, axis=1)


def halves(rows):
    return jnp.stack([rows[15 - d] for d in range(16)]), rows[16:]


def kernel(
    vol, w1_in, w2_in, b1_in, b2_in, back,
    landed, given, own, x, hid, res, w, w2t, rows8, bias, b1_s, b2_s, sem_b,
    sem_vol, sem_w, w_send, w_recv, b_send, b_recv, x_send, x_recv, s_send, s_recv, t_send, t_recv, u_send, u_recv,
    near_send, near_recv, far_send, far_recv, h_send, h_recv,
    in_send, in_recv, out_send, out_recv, sem_out,
):
    s = lax.axis_index("slab")
    k = lax.axis_index("chan")
    core = lax.rem(k, 2)
    chip = k // 2
    other = 1 - core
    sib = 2 * chip + other
    across = 2 * (1 - chip) + core
    diag = 2 * (1 - chip) + other
    mine = lax.rem(chip + s, 2)
    theirs = 1 - mine
    up, down = lax.rem(s + 1, SLABS), lax.rem(s + SLABS - 1, SLABS)
    y = lax.rem(s // 2, 4)
    odd = lax.rem(s // 8, 2)
    twin = 8 * (1 - 2 * odd)
    pair = s + 1 - 2 * lax.rem(s, 2)
    has_down, has_up = s > 0, s < SLABS - 1

    def y_peer(m):
        return s + 2 * (lax.rem(y + m, 4) - y)

    def chans(chan):
        return pl.ds(pl.multiple_of(chan * 32, 32), 32)

    ch = chans(k)
    far_ch = pl.ds(pl.multiple_of((1 - chip) * 64, 64), 64)

    def remote(src, dst, send, recv, slab, chan):
        return pltpu.make_async_remote_copy(
            src_ref=src, dst_ref=dst, send_sem=send, recv_sem=recv, device_id=(slab, chan), device_id_type=MESH
        )

    w[27] = jnp.zeros((128, 128), BF16)
    w[55] = jnp.zeros((128, 128), BF16)
    barrier = pltpu.get_barrier_semaphore()
    peers = [(s, sib), (s, across), (s, diag), (up, across), (down, across), (up, diag), (down, diag)]
    peers += [(y_peer(m), k) for m in (1, 2, 3)] + [(y_peer(m) + twin, k) for m in range(4)]
    for slab, chan in peers:
        pl.semaphore_signal(barrier, inc=1, device_id=(slab, chan), device_id_type=MESH)

    def own_w(n):
        return pltpu.make_async_copy((w1_in, w2_in)[n], w.at[pl.ds(28 * n, 27), ch, :], sem_w.at[n])

    def b_load(n):
        return pltpu.make_async_copy((b1_in, b2_in)[n], (b1_s, b2_s)[n], sem_b.at[n])

    def vol_copy(which, z):
        return pltpu.make_async_copy(vol.at[(mine, theirs)[which], z], landed.at[which, z], sem_vol.at[which, z])

    for n in range(2):
        b_load(n).start()
        own_w(n).start()
    for which, z in ((1, 0), (1, 1), (1, 2), (1, 3), (0, 0), (0, 3), (0, 1), (0, 2)):
        vol_copy(which, z).start()

    def blank():
        def blank_rows(i, carry):
            x[i, 18:20] = jnp.zeros((2, 128, 128), BF16)
            hid[i, 17] = jnp.zeros((128, 128), BF16)
            return carry

        lax.fori_loop(0, 6, blank_rows, 0)

        def blank_layer(layer):
            def row(i, carry):
                x[layer, i] = jnp.zeros((128, 128), BF16)
                hid[layer, i] = jnp.zeros((128, 128), BF16)
                return carry

            lax.fori_loop(0, 18, row, 0)

        @pl.when(jnp.logical_not(has_down))
        def _():
            blank_layer(0)

        @pl.when(jnp.logical_not(has_up))
        def _():
            blank_layer(5)

    at_row = lax.broadcasted_iota(jnp.int32, (8, 128), 0)
    at_lane = lax.broadcasted_iota(jnp.int32, (8, 128), 1) - 32 * k
    for n in range(2):
        b_load(n).wait()
    tile = jnp.zeros((8, 128), F32)
    for i in range(32):
        value = jnp.where(at_row == 0, b1_s[i], b2_s[i])
        tile = jnp.where(jnp.logical_and(at_lane == i, at_row < 2), value, tile)
    rows8[k] = tile

    def keep(which, z):
        vol_copy(which, z).wait()
        to = (own, given)[which]
        to[0, z], to[1, z] = halves(jnp.swapaxes(landed[which, z], 0, 1))

    for which, z in ((1, 0), (1, 1), (1, 2), (1, 3), (0, 0), (0, 3)):
        keep(which, z)
    pl.semaphore_wait(barrier, len(peers))

    def w_part(n, chan_from, quarter=None):
        taps = pl.ds(28 * n, 28) if quarter is None else pl.ds(28 * n + 7 * quarter, 7)
        return w.at[taps, chans(chan_from), :]

    def w_copy(i, receives=False):
        if i < 2:
            part, slab, chan = w_part(i, sib if receives else k), s, sib
        elif i < 4:
            part, slab, chan = w_part(i - 2, diag if receives else across), s, sib
        elif i == 4:
            part, slab, chan = w_part(odd, across if receives else k, y), pair, across
        else:
            m = i - 4 if i < 8 else i - 8
            n = odd if i < 8 or not receives else 1 - odd
            slab = y_peer(m) if i < 8 else y_peer(m) + twin
            part, chan = w_part(n, across, lax.rem(y + 4 - m, 4) if receives else y), k
        return remote(part, part, w_send.at[i], w_recv.at[i], slab, chan)

    def b_copy(i, receives=False):
        chan = (sib, across, diag)[i]
        part = rows8.at[chan if receives else k]
        return remote(part, part, b_send.at[i], b_recv.at[i], s, chan)

    for i in range(3):
        b_copy(i).start()
    for n in range(2):
        own_w(n).wait()
    w_copy(4).start()

    def x_copy(q, i):
        row, rows = CHUNKS[q]
        half, chan = ((core, across), (other, diag))[i]
        return remote(
            given.at[half, :, pl.ds(row, rows)], x.at[pl.ds(1, 4), pl.ds(row + 2, rows), ch, :],
            x_send.at[q, i], x_recv.at[q, i], s, chan,
        )

    def s_copy():
        return remote(own.at[other], x.at[pl.ds(1, 4), pl.ds(2, 16), ch, :], s_send, s_recv, s, sib)

    ENDS = ((3, 0, up, has_up, has_down), (0, 5, down, has_down, has_up))

    def near_copy(way, i):
        z, lands, slab = ENDS[way][:3]
        half, chan = ((core, across), (other, diag))[i]
        return remote(
            own.at[half, z], x.at[lands, pl.ds(2, 16), ch, :], near_send.at[way, i], near_recv.at[way, i], slab, chan
        )

    def far_copy(way, q):
        z, lands, slab = ENDS[way][:3]
        row, rows = CHUNKS[q]
        return remote(
            x.at[z + 1, pl.ds(row + 2, rows), far_ch, :], x.at[lands, pl.ds(row + 2, rows), far_ch, :],
            far_send.at[way, q], far_recv.at[way, q], slab, across,
        )

    def h_copy(way, q):
        z, lands, slab = ENDS[way][:3]
        rows = pl.ds(*HIDDEN[way][q])
        return remote(hid.at[z + 1, rows], hid.at[lands, rows], h_send.at[way, q], h_recv.at[way, q], slab, across)

    def t_copy(group, i):
        layers = (pl.ds(1, 4), 0, 5)[group]
        return remote(x.at[layers, 2 + i], x.at[layers, 1 - i], t_send.at[group, i], t_recv.at[group, i], s, sib)

    def u_copy(way):
        lands = ENDS[way][1]
        return remote(hid.at[lands, 1], hid.at[lands, 0], u_send.at[way], u_recv.at[way], s, sib)

    def start_ways(copy, way, *at):
        @pl.when(ENDS[way][3])
        def _():
            copy(way, *at).start()

    for q in range(4):
        for i in range(2):
            x_copy(q, i).start()
    for way in (1, 0):
        for i in range(2):
            start_ways(near_copy, way, i)
    for n in range(2):
        w_copy(n).start()
    for z in (1, 2):
        keep(0, z)
    s_copy().start()
    for z in range(4):
        x[z + 1, 2:18, ch, :] = own[core, z]
    blank()

    w_copy(4, True).wait_recv()
    for i in range(5, 12):
        w_copy(i).start()
    for i in range(3):
        b_copy(i, True).wait_recv()
    both = rows8[0] + rows8[1] + rows8[2] + rows8[3]
    for n in range(2):
        bias[n] = jnp.broadcast_to(both[n : n + 1], (128, 128)).T
    for i in range(5, 12):
        w_copy(i, True).wait_recv()
    for n in range(2):
        w_copy(n + 2).start()

    def turn(i, carry):
        w2t[i] = w[28 + i].T
        return carry

    s_copy().wait_recv()

    def o_copy(inner, z, q, i):
        chan = (sib, across, diag)[i]
        if inner:
            z, rows = pl.ds(1, 2), pl.ds(pl.multiple_of(4 * q, 4), 4)
            sems = in_send.at[q, i], in_recv.at[q, i]
        else:
            rows = pl.ds(pl.multiple_of(2 * q, 2), 2)
            sems = out_send.at[z // 3, q, i], out_recv.at[z // 3, q, i]
        return remote(res.at[z, rows, chans(chan), :], back.at[mine, z, core, rows], *sems, s, chan)

    def first(layers, row):
        weights, b = stacked(w, core), bias[0]
        for z in layers:
            for r in row:
                hid[z + 1, r], hid[z + 1, r + 1] = conv_rows(x, z, r, weights, b)

    def second(layers, row):
        weights, b = stacked(w2t, core), bias[1]
        for z in layers:
            for r in row:
                res[z, r], res[z, r + 1] = conv_rows(hid, z, r, weights, b)

    def last_row(layers):
        for z in layers:
            hid[z + 1, 17] = jnp.zeros((128, 128), BF16)

    def step(j, carry):
        @pl.when(j < 4)
        def _():
            for q in range(4):

                @pl.when(j == q)
                def _():
                    for i in range(2):
                        x_copy(q, i).wait_recv()
                    for way in (1, 0):
                        start_ways(far_copy, way, q)
                    if q == 0:
                        for i in range(2):
                            t_copy(0, i).start()
                        for n in (0, 2):
                            w_copy(n, True).wait_recv()

            first((1, 2), (4 * j + 2, 4 * j + 4))

            @pl.when(j == 0)
            def _():
                for i in range(2):
                    t_copy(0, i).wait_recv()
                first((1, 2), (0,))
                for n in (1, 3):
                    w_copy(n, True).wait_recv()
                lax.fori_loop(0, 27, turn, 0)

            @pl.when(j == 3)
            def _():
                last_row((1, 2))

        @pl.when(j >= 1)
        def _():
            i = j - 1
            for q in range(4):

                @pl.when(i == q)
                def _():
                    for way in (1, 0):

                        @pl.when(ENDS[way][4])
                        def _():
                            if q == 0:
                                for n in range(2):
                                    near_copy(way, n).wait_recv()
                            far_copy(way, q).wait_recv()
                            if q == 0:
                                for n in range(2):
                                    t_copy(1 + way, n).start()

            first((3, 0), (4 * i + 2, 4 * i + 4))

            @pl.when(i == 0)
            def _():
                for way in (1, 0):

                    @pl.when(ENDS[way][4])
                    def _():
                        for n in range(2):
                            t_copy(1 + way, n).wait_recv()

                first((3, 0), (0,))

            @pl.when(i == 3)
            def _():
                last_row((3, 0))

            for q in range(4):

                @pl.when(i == q)
                def _():
                    start_ways(h_copy, 0, q)
                    if q == 3:
                        for n in range(8):
                            start_ways(h_copy, 1, n)

            second((1, 2), (4 * i, 4 * i + 2))
            for n in (1, 2, 0):
                o_copy(True, None, i, n).start()

        return carry

    lax.fori_loop(0, 5, step, 0)

    def own_copy(z):
        return pltpu.make_async_copy(res.at[z, :, ch, :], back.at[mine, z, core], sem_out.at[z])

    def last_step(j, carry):
        z = 3 * (j // 8)
        i = lax.rem(j, 8)
        for way in range(2):
            for q in range((4, 8)[way]):

                @pl.when(jnp.logical_and(j == (2 * q, 8 + q)[way], ENDS[way][4]))
                def _():
                    h_copy(way, q).wait_recv()
                    if q == 0:
                        u_copy(way).start()
                        u_copy(way).wait_recv()

        second((z,), (2 * i,))
        for n in (1, 2, 0):
            o_copy(False, z, i, n).start()

        @pl.when(j == 7)
        def _():
            for q in range(4):
                for n in range(3):
                    o_copy(True, None, q, n).wait_recv()
            own_copy(1).start()
            own_copy(2).start()

        @pl.when(j == 13)
        def _():
            for q in range(8):
                for n in range(3):
                    o_copy(False, 0, q, n).wait_recv()
            own_copy(0).start()

        return carry

    lax.fori_loop(0, 16, last_step, 0)
    own_copy(3).start()
    for q in range(8):
        for n in range(3):
            o_copy(False, 3, q, n).wait_recv()

    for i in range(12):
        w_copy(i).wait_send()
    for i in range(3):
        b_copy(i).wait_send()
    s_copy().wait_send()
    for i in range(2):
        t_copy(0, i).wait_send()
    for way in range(2):

        @pl.when(ENDS[way][3])
        def _():
            for i in range(2):
                near_copy(way, i).wait_send()
            for q in range(4):
                far_copy(way, q).wait_send()
            for q in range((4, 8)[way]):
                h_copy(way, q).wait_send()

        @pl.when(ENDS[way][4])
        def _():
            u_copy(way).wait_send()
            for i in range(2):
                t_copy(1 + way, i).wait_send()

    for q in range(4):
        for i in range(2):
            x_copy(q, i).wait_send()
        for i in range(3):
            o_copy(True, None, q, i).wait_send()
    for q in range(8):
        for i in range(3):
            o_copy(False, 0, q, i).wait_send()
            o_copy(False, 3, q, i).wait_send()
    for z in range(4):
        own_copy(z).wait()


def finish(back, out):
    for z in range(4):
        rows = [back[0, z, 0, 15 - d] for d in range(16)] + [back[0, z, 1, d] for d in range(16)]
        out[0, z] = jnp.swapaxes(jnp.stack(rows), 0, 1)


def body(volume, first_kernel, first_bias, second_kernel, second_bias):
    w1 = jnp.transpose(first_kernel, (0, 1, 2, 4, 3)).reshape(27, 32, 128)
    w2 = second_kernel.reshape(27, 32, 128)
    dma = pltpu.SemaphoreType.DMA
    back = pl.pallas_call(
        kernel,
        out_shape=jax.ShapeDtypeStruct((2, 4, 2, 16, 32, 128), BF16),
        in_specs=[pl.BlockSpec(memory_space=pl.ANY)] * 3 + [pl.BlockSpec(memory_space=pl.ANY)] * 2,
        out_specs=pl.BlockSpec(memory_space=pl.ANY),
        scratch_shapes=[
            pltpu.VMEM((2, 4, 32, 32, 128), BF16),
            pltpu.VMEM((2, 4, 16, 32, 128), BF16),
            pltpu.VMEM((2, 4, 16, 32, 128), BF16),
            pltpu.VMEM((6, 20, 128, 128), BF16),
            pltpu.VMEM((6, 18, 128, 128), BF16),
            pltpu.VMEM((4, 16, 128, 128), BF16),
            pltpu.VMEM((56, 128, 128), BF16),
            pltpu.VMEM((27, 128, 128), BF16),
            pltpu.VMEM((4, 8, 128), F32),
            pltpu.VMEM((2, 128, 128), F32),
            pltpu.SMEM((32,), F32),
            pltpu.SMEM((32,), F32),
            dma((2,)),
            dma((2, 4)),
            dma((2,)),
            dma((12,)),
            dma((12,)),
            dma((3,)),
            dma((3,)),
            dma((4, 2)),
            dma((4, 2)),
            dma,
            dma,
            dma((3, 2)),
            dma((3, 2)),
            dma((2,)),
            dma((2,)),
            dma((2, 2)),
            dma((2, 2)),
            dma((2, 4)),
            dma((2, 4)),
            dma((2, 8)),
            dma((2, 8)),
            dma((4, 3)),
            dma((4, 3)),
            dma((2, 8, 3)),
            dma((2, 8, 3)),
            dma((4,)),
        ],
        name="two_convolutions",
        cost_estimate=pl.CostEstimate(flops=20_000_000_000, bytes_accessed=8_000_000, transcendentals=0),
        compiler_params=pltpu.CompilerParams(
            collective_id=0, has_side_effects=True, vmem_limit_bytes=60 * 1024 * 1024
        ),
    )(volume, w1, w2, first_bias, second_bias)
    return pl.pallas_call(
        finish,
        grid=(2, 1),
        out_shape=jax.ShapeDtypeStruct((2, 4, 32, 32, 128), BF16),
        in_specs=[pl.BlockSpec((1, 4, 2, 16, 32, 128), lambda b, z: (b, z, 0, 0, 0, 0))],
        out_specs=pl.BlockSpec((1, 4, 32, 32, 128), lambda b, z: (b, z, 0, 0, 0)),
        name="rows_to_channels",
        compiler_params=pltpu.CompilerParams(vmem_limit_bytes=16 * 1024 * 1024),
    )(back)


def solution(mesh):
    return jax.shard_map(
        body,
        mesh=mesh,
        in_specs=(
            P(None, "slab", "chan", None, None),
            P(None, None, None, None, "chan"),
            P("chan"),
            P(None, None, None, "chan", None),
            P("chan"),
        ),
        out_specs=P(None, "slab", "chan", None, None),
        check_vma=False,
    )
```

```python
import jax
import jax.numpy as jnp
from jax import lax
from jax.experimental import pallas as pl
from jax.experimental.pallas import tpu as pltpu
from jax.sharding import PartitionSpec as P

MESH = pl.DeviceIdType.MESH
SLABS = 32
BF16 = jnp.bfloat16
F32 = jnp.float32
CHUNKS = ((0, 6), (6, 4), (10, 4), (14, 2))
HIDDEN = (
    ((1, 5), (6, 4), (10, 4), (14, 3)),
    ((1, 3), (4, 2), (6, 2), (8, 2), (10, 2), (12, 2), (14, 2), (16, 1)),
)


def conv_rows(source, layer, row, weights, bias):
    taps = [
        jnp.concatenate([source[layer + a, row + c], source[layer + a, row + c + 1]], axis=1)
        for a in range(3)
        for c in range(3)
    ]
    sums = jnp.dot(weights, jnp.concatenate(taps, axis=0), preferred_element_type=F32)
    lane = lax.broadcasted_iota(jnp.int32, (128, 128), 1)
    outs = []
    for r in range(2):
        cols = slice(128 * r, 128 * r + 128)
        left = jnp.where(lane == 0, 0.0, pltpu.roll(sums[0:128, cols], 1, 1))
        right = jnp.where(lane == 127, 0.0, pltpu.roll(sums[256:384, cols], 127, 1))
        outs.append(jnp.maximum(sums[128:256, cols] + left + right + bias, 0.0).astype(BF16))
    return outs


def stacked(taps, core):
    parts = []
    for a in range(3):
        for c in range(3):
            at = 9 * a + 3 * (c + (1 - core) * (2 - 2 * c))
            parts.append(taps[pl.ds(at, 3)].reshape(384, 128))
    return jnp.concatenate(parts, axis=1)


def halves(rows):
    return jnp.stack([rows[15 - d] for d in range(16)]), rows[16:]


def kernel(
    vol, w1_in, w2_in, b1_in, b2_in, back,
    landed, given, own, x, hid, res, w, w2t, rows8, bias, b1_s, b2_s, sem_b,
    sem_vol, sem_w, w_send, w_recv, b_send, b_recv, x_send, x_recv, s_send, s_recv, t_send, t_recv, u_send, u_recv,
    near_send, near_recv, far_send, far_recv, h_send, h_recv,
    in_send, in_recv, out_send, out_recv, sem_out,
):
    s = lax.axis_index("slab")
    k = lax.axis_index("chan")
    core = lax.rem(k, 2)
    chip = k // 2
    other = 1 - core
    sib = 2 * chip + other
    across = 2 * (1 - chip) + core
    diag = 2 * (1 - chip) + other
    mine = lax.rem(chip + s, 2)
    theirs = 1 - mine
    up, down = lax.rem(s + 1, SLABS), lax.rem(s + SLABS - 1, SLABS)
    y = lax.rem(s // 2, 4)
    odd = lax.rem(s // 8, 2)
    twin = 8 * (1 - 2 * odd)
    pair = s + 1 - 2 * lax.rem(s, 2)
    has_down, has_up = s > 0, s < SLABS - 1

    def y_peer(m):
        return s + 2 * (lax.rem(y + m, 4) - y)

    def chans(chan):
        return pl.ds(pl.multiple_of(chan * 32, 32), 32)

    ch = chans(k)
    far_ch = pl.ds(pl.multiple_of((1 - chip) * 64, 64), 64)

    def remote(src, dst, send, recv, slab, chan):
        return pltpu.make_async_remote_copy(
            src_ref=src, dst_ref=dst, send_sem=send, recv_sem=recv, device_id=(slab, chan), device_id_type=MESH
        )

    w[27] = jnp.zeros((128, 128), BF16)
    w[55] = jnp.zeros((128, 128), BF16)
    barrier = pltpu.get_barrier_semaphore()
    peers = [(s, sib), (s, across), (s, diag), (up, across), (down, across), (up, diag), (down, diag)]
    peers += [(y_peer(m), k) for m in (1, 2, 3)] + [(y_peer(m) + twin, k) for m in range(4)]
    for slab, chan in peers:
        pl.semaphore_signal(barrier, inc=1, device_id=(slab, chan), device_id_type=MESH)

    def own_w(n):
        return pltpu.make_async_copy((w1_in, w2_in)[n], w.at[pl.ds(28 * n, 27), ch, :], sem_w.at[n])

    def b_load(n):
        return pltpu.make_async_copy((b1_in, b2_in)[n], (b1_s, b2_s)[n], sem_b.at[n])

    def vol_copy(which, z):
        return pltpu.make_async_copy(vol.at[(mine, theirs)[which], z], landed.at[which, z], sem_vol.at[which, z])

    for n in range(2):
        b_load(n).start()
        own_w(n).start()
    for which, z in ((1, 0), (1, 1), (1, 2), (1, 3), (0, 0), (0, 3), (0, 1), (0, 2)):
        vol_copy(which, z).start()

    def blank():
        def blank_rows(i, carry):
            x[i, 18:20] = jnp.zeros((2, 128, 128), BF16)
            hid[i, 17] = jnp.zeros((128, 128), BF16)
            return carry

        lax.fori_loop(0, 6, blank_rows, 0)

        def blank_layer(layer):
            def row(i, carry):
                x[layer, i] = jnp.zeros((128, 128), BF16)
                hid[layer, i] = jnp.zeros((128, 128), BF16)
                return carry

            lax.fori_loop(0, 18, row, 0)

        @pl.when(jnp.logical_not(has_down))
        def _():
            blank_layer(0)

        @pl.when(jnp.logical_not(has_up))
        def _():
            blank_layer(5)

    at_row = lax.broadcasted_iota(jnp.int32, (8, 128), 0)
    at_lane = lax.broadcasted_iota(jnp.int32, (8, 128), 1) - 32 * k
    for n in range(2):
        b_load(n).wait()
    tile = jnp.zeros((8, 128), F32)
    for i in range(32):
        value = jnp.where(at_row == 0, b1_s[i], b2_s[i])
        tile = jnp.where(jnp.logical_and(at_lane == i, at_row < 2), value, tile)
    rows8[k] = tile

    def keep(which, z):
        vol_copy(which, z).wait()
        to = (own, given)[which]
        to[0, z], to[1, z] = halves(jnp.swapaxes(landed[which, z], 0, 1))

    for which, z in ((1, 0), (1, 1), (1, 2), (1, 3), (0, 0), (0, 3)):
        keep(which, z)
    pl.semaphore_wait(barrier, len(peers))

    def w_part(n, chan_from, quarter=None):
        taps = pl.ds(28 * n, 28) if quarter is None else pl.ds(28 * n + 7 * quarter, 7)
        return w.at[taps, chans(chan_from), :]

    def w_copy(i, receives=False):
        if i < 2:
            part, slab, chan = w_part(i, sib if receives else k), s, sib
        elif i < 4:
            part, slab, chan = w_part(i - 2, diag if receives else across), s, sib
        elif i == 4:
            part, slab, chan = w_part(odd, across if receives else k, y), pair, across
        else:
            m = i - 4 if i < 8 else i - 8
            n = odd if i < 8 or not receives else 1 - odd
            slab = y_peer(m) if i < 8 else y_peer(m) + twin
            part, chan = w_part(n, across, lax.rem(y + 4 - m, 4) if receives else y), k
        return remote(part, part, w_send.at[i], w_recv.at[i], slab, chan)

    def b_copy(i, receives=False):
        chan = (sib, across, diag)[i]
        part = rows8.at[chan if receives else k]
        return remote(part, part, b_send.at[i], b_recv.at[i], s, chan)

    for i in range(3):
        b_copy(i).start()
    for n in range(2):
        own_w(n).wait()
    w_copy(4).start()

    def x_copy(q, i):
        row, rows = CHUNKS[q]
        half, chan = ((core, across), (other, diag))[i]
        return remote(
            given.at[half, :, pl.ds(row, rows)], x.at[pl.ds(1, 4), pl.ds(row + 2, rows), ch, :],
            x_send.at[q, i], x_recv.at[q, i], s, chan,
        )

    def s_copy():
        return remote(own.at[other], x.at[pl.ds(1, 4), pl.ds(2, 16), ch, :], s_send, s_recv, s, sib)

    ENDS = ((3, 0, up, has_up, has_down), (0, 5, down, has_down, has_up))

    def near_copy(way, i):
        z, lands, slab = ENDS[way][:3]
        half, chan = ((core, across), (other, diag))[i]
        return remote(
            own.at[half, z], x.at[lands, pl.ds(2, 16), ch, :], near_send.at[way, i], near_recv.at[way, i], slab, chan
        )

    def far_copy(way, q):
        z, lands, slab = ENDS[way][:3]
        row, rows = CHUNKS[q]
        return remote(
            x.at[z + 1, pl.ds(row + 2, rows), far_ch, :], x.at[lands, pl.ds(row + 2, rows), far_ch, :],
            far_send.at[way, q], far_recv.at[way, q], slab, across,
        )

    def h_copy(way, q):
        z, lands, slab = ENDS[way][:3]
        rows = pl.ds(*HIDDEN[way][q])
        return remote(hid.at[z + 1, rows], hid.at[lands, rows], h_send.at[way, q], h_recv.at[way, q], slab, across)

    def t_copy(group, i):
        layers = (pl.ds(1, 4), 0, 5)[group]
        return remote(x.at[layers, 2 + i], x.at[layers, 1 - i], t_send.at[group, i], t_recv.at[group, i], s, sib)

    def u_copy(way):
        lands = ENDS[way][1]
        return remote(hid.at[lands, 1], hid.at[lands, 0], u_send.at[way], u_recv.at[way], s, sib)

    def start_ways(copy, way, *at):
        @pl.when(ENDS[way][3])
        def _():
            copy(way, *at).start()

    for q in range(4):
        for i in range(2):
            x_copy(q, i).start()
    for way in (1, 0):
        for i in range(2):
            start_ways(near_copy, way, i)
    for n in range(2):
        w_copy(n).start()
    for z in (1, 2):
        keep(0, z)
    s_copy().start()
    for z in range(4):
        x[z + 1, 2:18, ch, :] = own[core, z]
    blank()

    w_copy(4, True).wait_recv()
    for i in range(5, 12):
        w_copy(i).start()
    for i in range(3):
        b_copy(i, True).wait_recv()
    both = rows8[0] + rows8[1] + rows8[2] + rows8[3]
    for n in range(2):
        bias[n] = jnp.broadcast_to(both[n : n + 1], (128, 128)).T
    for i in range(5, 12):
        w_copy(i, True).wait_recv()
    for n in range(2):
        w_copy(n + 2).start()

    def turn(i, carry):
        w2t[i] = w[28 + i].T
        return carry

    s_copy().wait_recv()

    def o_copy(inner, z, q, i):
        chan = (sib, across, diag)[i]
        if inner:
            z, rows = pl.ds(1, 2), pl.ds(pl.multiple_of(4 * q, 4), 4)
            sems = in_send.at[q, i], in_recv.at[q, i]
        else:
            rows = pl.ds(pl.multiple_of(2 * q, 2), 2)
            sems = out_send.at[z // 3, q, i], out_recv.at[z // 3, q, i]
        return remote(res.at[z, rows, chans(chan), :], back.at[mine, z, core, rows], *sems, s, chan)

    def first(layers, row):
        weights, b = stacked(w, core), bias[0]
        for z in layers:
            for r in row:
                hid[z + 1, r], hid[z + 1, r + 1] = conv_rows(x, z, r, weights, b)

    def second(layers, row):
        weights, b = stacked(w2t, core), bias[1]
        for z in layers:
            for r in row:
                res[z, r], res[z, r + 1] = conv_rows(hid, z, r, weights, b)

    def last_row(layers):
        for z in layers:
            hid[z + 1, 17] = jnp.zeros((128, 128), BF16)

    def step(j, carry):
        @pl.when(j < 4)
        def _():
            for q in range(4):

                @pl.when(j == q)
                def _():
                    for i in range(2):
                        x_copy(q, i).wait_recv()
                    for way in (1, 0):
                        start_ways(far_copy, way, q)
                    if q == 0:
                        for i in range(2):
                            t_copy(0, i).start()
                        for n in (0, 2):
                            w_copy(n, True).wait_recv()

            first((1, 2), (4 * j + 2, 4 * j + 4))

            @pl.when(j == 0)
            def _():
                for i in range(2):
                    t_copy(0, i).wait_recv()
                first((1, 2), (0,))
                for n in (1, 3):
                    w_copy(n, True).wait_recv()
                lax.fori_loop(0, 27, turn, 0)

            @pl.when(j == 3)
            def _():
                last_row((1, 2))

        @pl.when(j >= 1)
        def _():
            i = j - 1
            for q in range(4):

                @pl.when(i == q)
                def _():
                    for way in (1, 0):

                        @pl.when(ENDS[way][4])
                        def _():
                            if q == 0:
                                for n in range(2):
                                    near_copy(way, n).wait_recv()
                            far_copy(way, q).wait_recv()
                            if q == 0:
                                for n in range(2):
                                    t_copy(1 + way, n).start()

            first((3, 0), (4 * i + 2, 4 * i + 4))

            @pl.when(i == 0)
            def _():
                for way in (1, 0):

                    @pl.when(ENDS[way][4])
                    def _():
                        for n in range(2):
                            t_copy(1 + way, n).wait_recv()

                first((3, 0), (0,))

            @pl.when(i == 3)
            def _():
                last_row((3, 0))

            for q in range(4):

                @pl.when(i == q)
                def _():
                    start_ways(h_copy, 0, q)
                    for n in {2: range(3), 3: range(3, 8)}.get(q, ()):
                        start_ways(h_copy, 1, n)

            second((1, 2), (4 * i, 4 * i + 2))
            for n in (1, 2, 0):
                o_copy(True, None, i, n).start()

        return carry

    lax.fori_loop(0, 5, step, 0)

    def own_copy(z):
        return pltpu.make_async_copy(res.at[z, :, ch, :], back.at[mine, z, core], sem_out.at[z])

    def last_step(j, carry):
        z = 3 * (j // 8)
        i = lax.rem(j, 8)
        for way in range(2):
            for q in range((4, 8)[way]):

                @pl.when(jnp.logical_and(j == (2 * q, 8 + q)[way], ENDS[way][4]))
                def _():
                    h_copy(way, q).wait_recv()
                    if q == 0:
                        u_copy(way).start()
                        u_copy(way).wait_recv()

        second((z,), (2 * i,))
        for n in (1, 2, 0):
            o_copy(False, z, i, n).start()

        @pl.when(j == 7)
        def _():
            for q in range(4):
                for n in range(3):
                    o_copy(True, None, q, n).wait_recv()
            own_copy(1).start()
            own_copy(2).start()

        @pl.when(j == 13)
        def _():
            for q in range(8):
                for n in range(3):
                    o_copy(False, 0, q, n).wait_recv()
            own_copy(0).start()

        return carry

    lax.fori_loop(0, 16, last_step, 0)
    own_copy(3).start()
    for q in range(8):
        for n in range(3):
            o_copy(False, 3, q, n).wait_recv()

    for i in range(12):
        w_copy(i).wait_send()
    for i in range(3):
        b_copy(i).wait_send()
    s_copy().wait_send()
    for i in range(2):
        t_copy(0, i).wait_send()
    for way in range(2):

        @pl.when(ENDS[way][3])
        def _():
            for i in range(2):
                near_copy(way, i).wait_send()
            for q in range(4):
                far_copy(way, q).wait_send()
            for q in range((4, 8)[way]):
                h_copy(way, q).wait_send()

        @pl.when(ENDS[way][4])
        def _():
            u_copy(way).wait_send()
            for i in range(2):
                t_copy(1 + way, i).wait_send()

    for q in range(4):
        for i in range(2):
            x_copy(q, i).wait_send()
        for i in range(3):
            o_copy(True, None, q, i).wait_send()
    for q in range(8):
        for i in range(3):
            o_copy(False, 0, q, i).wait_send()
            o_copy(False, 3, q, i).wait_send()
    for z in range(4):
        own_copy(z).wait()


def finish(back, out):
    for z in range(4):
        rows = [back[0, z, 0, 15 - d] for d in range(16)] + [back[0, z, 1, d] for d in range(16)]
        out[0, z] = jnp.swapaxes(jnp.stack(rows), 0, 1)


def body(volume, first_kernel, first_bias, second_kernel, second_bias):
    w1 = jnp.transpose(first_kernel, (0, 1, 2, 4, 3)).reshape(27, 32, 128)
    w2 = second_kernel.reshape(27, 32, 128)
    dma = pltpu.SemaphoreType.DMA
    back = pl.pallas_call(
        kernel,
        out_shape=jax.ShapeDtypeStruct((2, 4, 2, 16, 32, 128), BF16),
        in_specs=[pl.BlockSpec(memory_space=pl.ANY)] * 3 + [pl.BlockSpec(memory_space=pl.ANY)] * 2,
        out_specs=pl.BlockSpec(memory_space=pl.ANY),
        scratch_shapes=[
            pltpu.VMEM((2, 4, 32, 32, 128), BF16),
            pltpu.VMEM((2, 4, 16, 32, 128), BF16),
            pltpu.VMEM((2, 4, 16, 32, 128), BF16),
            pltpu.VMEM((6, 20, 128, 128), BF16),
            pltpu.VMEM((6, 18, 128, 128), BF16),
            pltpu.VMEM((4, 16, 128, 128), BF16),
            pltpu.VMEM((56, 128, 128), BF16),
            pltpu.VMEM((27, 128, 128), BF16),
            pltpu.VMEM((4, 8, 128), F32),
            pltpu.VMEM((2, 128, 128), F32),
            pltpu.SMEM((32,), F32),
            pltpu.SMEM((32,), F32),
            dma((2,)),
            dma((2, 4)),
            dma((2,)),
            dma((12,)),
            dma((12,)),
            dma((3,)),
            dma((3,)),
            dma((4, 2)),
            dma((4, 2)),
            dma,
            dma,
            dma((3, 2)),
            dma((3, 2)),
            dma((2,)),
            dma((2,)),
            dma((2, 2)),
            dma((2, 2)),
            dma((2, 4)),
            dma((2, 4)),
            dma((2, 8)),
            dma((2, 8)),
            dma((4, 3)),
            dma((4, 3)),
            dma((2, 8, 3)),
            dma((2, 8, 3)),
            dma((4,)),
        ],
        name="two_convolutions",
        cost_estimate=pl.CostEstimate(flops=20_000_000_000, bytes_accessed=8_000_000, transcendentals=0),
        compiler_params=pltpu.CompilerParams(
            collective_id=0, has_side_effects=True, vmem_limit_bytes=60 * 1024 * 1024
        ),
    )(volume, w1, w2, first_bias, second_bias)
    return pl.pallas_call(
        finish,
        grid=(2, 1),
        out_shape=jax.ShapeDtypeStruct((2, 4, 32, 32, 128), BF16),
        in_specs=[pl.BlockSpec((1, 4, 2, 16, 32, 128), lambda b, z: (b, z, 0, 0, 0, 0))],
        out_specs=pl.BlockSpec((1, 4, 32, 32, 128), lambda b, z: (b, z, 0, 0, 0)),
        name="rows_to_channels",
        compiler_params=pltpu.CompilerParams(vmem_limit_bytes=16 * 1024 * 1024),
    )(back)


def solution(mesh):
    return jax.shard_map(
        body,
        mesh=mesh,
        in_specs=(
            P(None, "slab", "chan", None, None),
            P(None, None, None, None, "chan"),
            P("chan"),
            P(None, None, None, "chan", None),
            P("chan"),
        ),
        out_specs=P(None, "slab", "chan", None, None),
        check_vma=False,
    )
```
